32 devices in a mesh: wide: 4 (over y, x), narrow: 8 (over z, core).
Axes of the slice: x: 2, y: 2, z: 4, core: 2. Of those that a mesh axis runs over, the one named last changes fastest.
Arguments:
- positions: float32 [384, 3, 256], P(('wide', 'narrow')), may hold values from 6 to 18
- forces: float32 [384, 256], P(('wide', 'narrow')), may hold values from -0.6 to 0.6
- counts: int32 [384], P(('wide', 'narrow')), may hold values from 0 to 256, as said below
- anchors: int32 [3, 384], P(None, ('wide', 'narrow')), may hold values from 0 to 1023, as said below
- helpers: int32 [384, 1], P(('wide', 'narrow')), may hold values from 0 to 7, as said below
Outputs:
- spectrum: float32 [2, 32, 1024, 1024], P(None, 'wide', 'narrow')
- helper_load: float32 [4, 8], P('wide', 'narrow')
The draws below stay inside these ranges and needn't reach their ends.
Inputs may be any that keep to these rules, and one draw needn't show every extreme that they name: `counts`: within each device's 12 bins the bins with a nonzero count come first; some device has all its bins nonzero. `helpers`: within each device's 12 bins at most 2 bins name the same helper. anchors[0] < 8, anchors[1] < 128, anchors[2] < 1024.
All inputs are finite; a program needn't handle non-finite values.
Results may differ from the reference program's by a relative error of at most 0.0054.
Values may be sent and summed in bfloat16 or wider, within the bound.
A program may use at most 128 MiB of HBM per device.

```python
import math
import jax
import jax.numpy as jnp
from jax import lax

XS = 8
NY = 1024
NZ = 1024
PATCH = 24
BIN = 256
BINS_DEV = 12
BINS = 384
N_WIDE = 4
N_NARROW = 8
DEVICES = 32


def draw_positions(key, part):
    first_key, second_key, third_key = jax.random.split(key, 3)
    lowest = float(PATCH // 4)
    topmost = float(3 * PATCH // 4)
    array_dims = (BINS_DEV * DEVICES, 3, BIN)
    scattered = jax.random.uniform(first_key, array_dims, jnp.float32, lowest, topmost)
    chooser = jax.random.randint(second_key, array_dims, 0, 8)
    sided = jax.random.randint(third_key, array_dims, 0, 2)
    at_ends = jnp.where(sided == 0, jnp.float32(lowest), jnp.float32(topmost))
    end_share = 2
    return jnp.where(chooser < end_share, at_ends, scattered).astype(jnp.float32)


def draw_counts(key, part):
    first_key, second_key, third_key = jax.random.split(key, 3)
    level = jax.random.randint(first_key, (DEVICES,), 0, 8)
    living = jnp.maximum(1, BINS_DEV * level ** 3 // 343)
    filled = jax.random.randint(second_key, (), 0, DEVICES)
    living = jnp.where(jnp.arange(DEVICES) == filled, BINS_DEV, living)
    ordinal = jnp.arange(BINS_DEV)
    alive = ordinal[None, :] < living[:, None]
    sizes = jax.random.randint(third_key, (DEVICES, BINS_DEV), 1, BIN + 1)
    return jnp.where(alive, sizes, 0).reshape(-1).astype(jnp.int32)


def draw_anchors(key, part):
    limits = jnp.array([XS, NY // N_NARROW, NZ], jnp.int32)
    return jax.random.randint(key, (3, BINS_DEV * DEVICES), 0, limits[:, None]).astype(jnp.int32)


def draw_helpers(key, part):
    device_keys = jax.random.split(key, DEVICES)
    slot_total = N_NARROW * ((BINS_DEV + N_NARROW - 1) // N_NARROW)
    shuffled = jax.vmap(lambda single: jax.random.permutation(single, slot_total))(device_keys)
    chosen = shuffled[:, :BINS_DEV] // ((BINS_DEV + N_NARROW - 1) // N_NARROW)
    return chosen.reshape(BINS_DEV * DEVICES, 1).astype(jnp.int32)


def steps_of(key, dims, pieces, least, largest):
    gain, own = 1.0, jax.random.fold_in(key, 6)
    for dim, blocks in pieces:
        steps = jnp.exp(jax.random.uniform(jax.random.fold_in(own, dim), (blocks,), jnp.float32, least / len(pieces), largest / len(pieces)))
        gain = gain * jnp.repeat(steps, dims[dim] // blocks).reshape([-1 if axis == dim else 1 for axis in range(len(dims))])
    return gain


def centred(key, shape, scale, limit, pieces=(), kind=jnp.bfloat16):
    entries = jax.random.normal(key, shape, jnp.float32) * scale
    if len(pieces) > 0:
        entries = steps_of(key, shape, pieces, -0.22, 0.18) * entries
    return jnp.clip(entries, min=-limit, max=limit).astype(kind)


def setup_inputs(seed: int = 0) -> dict:
    key_list = jax.random.split(jax.random.key(seed), 6)
    positions = draw_positions(jax.random.fold_in(key_list[5], 71), 0)
    forces = centred(key_list[1], (BINS, BIN), 0.1, 0.6, ((0, 32),), jnp.float32)
    counts = draw_counts(jax.random.fold_in(key_list[5], 71), 0)
    anchors = draw_anchors(jax.random.fold_in(key_list[5], 71), 0)
    helpers = draw_helpers(jax.random.fold_in(key_list[5], 71), 0)
    return dict(positions=positions, forces=forces, counts=counts, anchors=anchors, helpers=helpers)


spread_rate = 0.08
two_pi = 2.0 * math.pi

def bin_patch(places, strength, number):
    cell_index = jnp.arange(PATCH, dtype=jnp.float32)
    living = jnp.arange(BIN, dtype=jnp.int32) < number
    weights = jnp.where(living, strength, jnp.zeros_like(strength))
    along_x = jnp.exp(-spread_rate * (cell_index[None, :] - places[0][:, None]) ** 2)
    along_y = jnp.exp(-spread_rate * (cell_index[None, :] - places[1][:, None]) ** 2)
    along_z = jnp.exp(-spread_rate * (cell_index[None, :] - places[2][:, None]) ** 2)
    left_side = weights[:, None] * along_x
    right_side = (along_y[:, :, None] * along_z[:, None, :]).reshape(BIN, PATCH * PATCH)
    return jnp.dot(left_side.T, right_side, precision=lax.Precision.HIGHEST)

def unchanged(volume):
    return volume

def dft_tables(length, columns):
    ordinal = jnp.arange(length, dtype=jnp.int32)
    phase = ordinal[:, None] * columns[None, :] % length
    angle = phase.astype(jnp.float32) * (two_pi / length)
    norm_scale = 1.0 / math.sqrt(length)
    return ((jnp.cos(angle) * norm_scale).astype(jnp.bfloat16), (jnp.sin(angle) * norm_scale).astype(jnp.bfloat16))

def reference(positions, forces, counts, anchors, helpers):
    width_x = XS * N_WIDE
    own_rows = NY // N_NARROW
    total_bins = BINS_DEV * N_WIDE * N_NARROW
    padded = jnp.zeros((width_x + PATCH, NY + PATCH, NZ + PATCH), jnp.float32)

    def place(bin_index, padded):
        bin_index = jnp.asarray(bin_index).astype(jnp.int32)
        device = bin_index // BINS_DEV
        corner = (device // N_NARROW * XS + anchors[0, bin_index], device % N_NARROW * own_rows + anchors[1, bin_index], anchors[2, bin_index])
        corner = tuple((entry.astype(jnp.int32) for entry in corner))

        def added(volume):
            patch = bin_patch(positions[bin_index], forces[bin_index], counts[bin_index])
            rounded = lax.optimization_barrier(patch.astype(jnp.bfloat16)).astype(jnp.float32)
            rounded = rounded.reshape(PATCH, PATCH, PATCH)
            region = lax.dynamic_slice(volume, corner, (PATCH, PATCH, PATCH))
            return lax.dynamic_update_slice(volume, region + rounded, corner)
        return lax.cond(counts[bin_index] > 0, added, unchanged, padded)
    padded = lax.fori_loop(0, total_bins, place, padded)
    folded = padded[:width_x].at[:PATCH].add(padded[width_x:])
    folded = folded[:, :NY].at[:, :PATCH].add(folded[:, NY:])
    folded = folded[:, :, :NZ].at[:, :, :PATCH].add(folded[:, :, NZ:])
    block_rows = NZ // N_NARROW
    slot_index = jnp.arange(NZ, dtype=jnp.int32)
    column_order = (slot_index % block_rows * N_NARROW + slot_index // block_rows).astype(jnp.int32)
    cos_z, sin_z = dft_tables(NZ, column_order)
    cos_y, sin_y = dft_tables(NY, jnp.arange(NY, dtype=jnp.int32))

    def transform(plane):
        half = plane.astype(jnp.bfloat16)
        z_real = jnp.dot(half, cos_z, preferred_element_type=jnp.float32).astype(jnp.bfloat16)
        z_imag = (-jnp.dot(half, sin_z, preferred_element_type=jnp.float32)).astype(jnp.bfloat16)
        out_real = jnp.dot(z_real.T, cos_y, preferred_element_type=jnp.float32) + jnp.dot(z_imag.T, sin_y, preferred_element_type=jnp.float32)
        out_imag = jnp.dot(z_imag.T, cos_y, preferred_element_type=jnp.float32) - jnp.dot(z_real.T, sin_y, preferred_element_type=jnp.float32)
        return jnp.stack([out_real, out_imag])
    spectra = lax.map(transform, folded)
    spectrum = jnp.moveaxis(spectra, 1, 0).astype(jnp.float32)
    group_help = helpers.reshape(N_WIDE, BINS_DEV * N_NARROW)
    group_count = counts.reshape(N_WIDE, BINS_DEV * N_NARROW).astype(jnp.float32)
    matches = group_help[:, :, None] == jnp.arange(N_NARROW, dtype=jnp.int32)[None, None, :]
    helper_load = lax.optimization_barrier(jnp.sum(jnp.where(matches, group_count[:, :, None], jnp.zeros_like(group_count)[:, :, None]), axis=1)) / BIN
    return (spectrum, helper_load.astype(jnp.float32))
```

```python
import math

import jax
import jax.numpy as jnp
import numpy as np
from jax import lax
from jax.experimental import pallas as pl
from jax.experimental.pallas import tpu as pltpu
from jax.sharding import PartitionSpec as P

XS = 8
NY = 1024
NZ = 1024
PATCH = 24
SPLIT = 4
WINDOW = 32
TOGETHER = 4
META_ROWS = 8
LANES = 128

spread_rate = 0.08
two_pi = 2.0 * math.pi


def y_tables():
    points = NY // SPLIT
    y = np.arange(points)[None, :] * SPLIT + np.arange(SPLIT)[:, None]
    phase = (y[:, :, None] * np.arange(points)[None, None, :]) % NY
    angle = phase * (two_pi / NY)
    cos = np.cos(angle) / math.sqrt(NY)
    sin = np.sin(angle) / math.sqrt(NY)
    upper = np.concatenate([cos, -sin], axis=2)
    lower = np.concatenate([sin, cos], axis=2)
    return np.concatenate([upper, lower], axis=1).astype(np.float32).astype(jnp.bfloat16)


def z_table(block, count, me):
    frequency = jnp.arange(block, dtype=jnp.int32) * count + me
    phase = frequency[:, None] * jnp.arange(block, dtype=jnp.int32)[None, :] % NZ
    angle = phase.astype(jnp.float32) * (two_pi / NZ)
    cos = jnp.cos(angle) / math.sqrt(NZ)
    sin = jnp.sin(angle) / math.sqrt(NZ)
    top = jnp.concatenate([cos, sin], axis=1)
    bottom = jnp.concatenate([-sin, cos], axis=1)
    return jnp.concatenate([top, bottom], axis=0).astype(jnp.bfloat16)


def spectrum_kernel(
    live, xoff, ycell, zcell, turn, parts, ztab, ytab, out, folded, order, rows,
    *, bins, block, count, stride
):
    step = pl.program_id(0)
    window = WINDOW
    particles = parts.shape[1]

    @pl.when(step == 0)
    def _():
        folded[...] = jnp.zeros_like(folded)

        def per_device(device, total):
            def per_bin(b, total):
                order[total] = device * bins + b
                rows[total] = device * stride + b * 4
                return total + 1

            return lax.fori_loop(0, live[device], per_bin, total)

        total = lax.fori_loop(0, live.shape[0], per_device, 0)
        for extra in range(TOGETHER):
            order[total + extra] = 0
            rows[total + extra] = 0

        def gauss(cell, place):
            away = cell.astype(jnp.float32) - place
            return jnp.exp(-spread_rate * (away * away))

        def product(k):
            b, r = order[k], rows[k]
            x0, y0, z0 = xoff[b], ycell[b], zcell[b]
            px = parts[pl.ds(r, 1), :]
            py = parts[pl.ds(r + 1, 1), :]
            pz = parts[pl.ds(r + 2, 1), :]
            force = parts[pl.ds(r + 3, 1), :]
            force = jnp.where(k < total, force, jnp.zeros_like(force))
            xi = lax.broadcasted_iota(jnp.int32, (XS, particles), 0) + x0
            along_x = jnp.where((xi >= 0) & (xi < PATCH), gauss(xi, px) * force, 0.0)
            yi = lax.broadcasted_iota(jnp.int32, (window, particles), 0) - (y0 & 7)
            along_y = jnp.where((yi >= 0) & (yi < PATCH), gauss(yi, py), 0.0)
            left = along_x[:, None, :] * along_y[None, :, :]
            left = left.reshape(XS * window, particles).astype(jnp.bfloat16)
            at = z0 & (block - 1)
            s0 = z0 // block
            s1 = (s0 + 1) & (count - 1)
            zrow = lax.broadcasted_iota(jnp.int32, (block, particles), 0)
            zi = (zrow - at) & (block - 1)
            along_z = jnp.where(zi < PATCH, gauss(zi, pz), 0.0)
            first = zrow >= at
            real = along_z * jnp.where(first, turn[s0], turn[s1])
            imag = along_z * jnp.where(first, turn[count + s0], turn[count + s1])
            right = jnp.concatenate([real, imag], axis=0).astype(jnp.bfloat16)
            value = lax.dot_general(
                left, right, (((1,), (1,)), ((), ())), preferred_element_type=jnp.float32
            )
            return value.reshape(XS, window, 2 * block), pl.multiple_of(y0 // 8 * 8, 8)

        def group(g, carry):
            results = [product(g * TOGETHER + u) for u in range(TOGETHER)]
            for value, base in results:
                for h in range(2 * block // LANES):
                    folded[h, :, pl.ds(base, window), :] += value[:, :, h * LANES : (h + 1) * LANES]
            return carry

        lax.fori_loop(0, (total + TOGETHER - 1) // TOGETHER, group, 0)
        folded[:, :, :window, :] += folded[:, :, NY:, :]

    points = NY // SPLIT
    terms = []
    for t in range(SPLIT):
        lines = jnp.concatenate(
            [
                folded[h, step, pl.ds(t, points, stride=SPLIT), :].astype(jnp.bfloat16)
                for h in range(2 * block // LANES)
            ],
            axis=1,
        )
        along = lax.dot_general(
            ztab[...], lines, (((1,), (1,)), ((), ())), preferred_element_type=jnp.float32
        ).astype(jnp.bfloat16)
        along = jnp.concatenate([along[:block], along[block:]], axis=1)
        terms.append(jnp.dot(along, ytab[t], preferred_element_type=jnp.float32))
    plus, minus = terms[0] + terms[2], terms[0] - terms[2]
    odd_plus, odd_minus = terms[1] + terms[3], terms[1] - terms[3]
    low = plus + odd_plus
    high = plus - odd_plus
    out[0, 0, :, 0:points] = low[:, :points]
    out[1, 0, :, 0:points] = low[:, points:]
    out[0, 0, :, 2 * points : 3 * points] = high[:, :points]
    out[1, 0, :, 2 * points : 3 * points] = high[:, points:]
    out[0, 0, :, points : 2 * points] = minus[:, :points] + odd_minus[:, points:]
    out[1, 0, :, points : 2 * points] = minus[:, points:] - odd_minus[:, :points]
    out[0, 0, :, 3 * points :] = minus[:, :points] - odd_minus[:, points:]
    out[1, 0, :, 3 * points :] = minus[:, points:] + odd_minus[:, :points]


def body(positions, forces, counts, anchors, helpers):
    bins, _, particles = positions.shape
    count = lax.axis_size("narrow")
    wide = lax.axis_size("wide")
    devices = count * wide
    me_wide = lax.axis_index("wide")
    me = lax.axis_index("narrow")
    block = NZ // count
    own_rows = NY // count
    ghost_slabs = (PATCH + XS - 2) // XS
    stride = bins * 4 + META_ROWS

    live_mask = jnp.arange(particles, dtype=jnp.int32)[None, :] < counts[:, None]
    masked = jnp.where(live_mask, forces, jnp.zeros_like(forces))
    own = jnp.concatenate([positions, masked[:, None, :]], axis=1).reshape(bins * 4, particles)
    facts = jnp.concatenate([counts[None, :], anchors, helpers.T], axis=0).astype(jnp.float32)
    facts = jnp.pad(facts, ((0, META_ROWS - facts.shape[0]), (0, particles - bins)))
    parts = lax.all_gather(
        jnp.concatenate([own, facts], axis=0), ("wide", "narrow"), axis=0, tiled=True
    )
    facts = parts.reshape(devices, stride, particles)[:, bins * 4 : bins * 4 + 5, :bins]
    facts = facts.astype(jnp.int32)
    all_counts = facts[:, 0]
    device = jnp.arange(devices, dtype=jnp.int32)
    slabs = jnp.mod(me_wide - device // count, wide)
    live = jnp.sum((all_counts > 0).astype(jnp.int32), axis=1)
    live = jnp.where(slabs <= ghost_slabs, live, 0)
    xoff = (slabs[:, None] * XS - facts[:, 1]).reshape(-1)
    ycell = ((device % count)[:, None] * own_rows + facts[:, 2]).reshape(-1)
    zcell = facts[:, 3].reshape(-1)
    group = (device // count == me_wide)[:, None] & (facts[:, 4] == me)
    load = jnp.sum(jnp.where(group, all_counts, 0)).astype(jnp.float32) / particles
    quarter = jnp.arange(count, dtype=jnp.int32) * me % count
    angle = quarter.astype(jnp.float32) * (two_pi / count)
    turn = jnp.concatenate([jnp.cos(angle), -jnp.sin(angle)])
    ytab = jnp.asarray(y_tables())
    ztab = z_table(block, count, me)

    smem = pl.BlockSpec(memory_space=pltpu.SMEM)
    points = NY // SPLIT
    spectrum = pl.pallas_call(
        lambda *refs: spectrum_kernel(
            *refs, bins=bins, block=block, count=count, stride=stride
        ),
        grid=(XS,),
        in_specs=[smem] * 5
        + [
            pl.BlockSpec(parts.shape, lambda x: (0, 0)),
            pl.BlockSpec(ztab.shape, lambda x: (0, 0)),
            pl.BlockSpec(ytab.shape, lambda x: (0, 0, 0)),
        ],
        out_specs=pl.BlockSpec((2, 1, block, NY), lambda x: (0, x, 0, 0)),
        out_shape=jax.ShapeDtypeStruct((2, XS, block, NY), jnp.float32),
        scratch_shapes=[
            pltpu.VMEM((2 * block // LANES, XS, NY + WINDOW, LANES), jnp.float32),
            pltpu.SMEM((devices * bins + TOGETHER,), jnp.int32),
            pltpu.SMEM((devices * bins + TOGETHER,), jnp.int32),
        ],
        compiler_params=pltpu.CompilerParams(
            dimension_semantics=("arbitrary",), vmem_limit_bytes=60 * 1024 * 1024
        ),
        name="spread_and_transform",
    )(live, xoff, ycell, zcell, turn, parts, ztab, ytab)
    return (spectrum, load.reshape(1, 1))


def solution(mesh):
    return jax.shard_map(
        body,
        mesh=mesh,
        in_specs=(
            P(("wide", "narrow"), None, None),
            P(("wide", "narrow"), None),
            P(("wide", "narrow")),
            P(None, ("wide", "narrow")),
            P(("wide", "narrow"), None),
        ),
        out_specs=(P(None, "wide", "narrow", None), P("wide", "narrow")),
        check_vma=False,
    )
```

```python
import math

import jax
import jax.numpy as jnp
import numpy as np
from jax import lax
from jax.experimental import pallas as pl
from jax.experimental.pallas import tpu as pltpu
from jax.sharding import PartitionSpec as P

XS = 8
NY = 1024
NZ = 1024
PATCH = 24
SPLIT = 4
WINDOW = 32
TOGETHER = 4
META_ROWS = 8
LANES = 128

spread_rate = 0.08
two_pi = 2.0 * math.pi


def y_tables():
    points = NY // SPLIT
    y = np.arange(points)[None, :] * SPLIT + np.arange(SPLIT)[:, None]
    phase = (y[:, :, None] * np.arange(points)[None, None, :]) % NY
    angle = phase * (two_pi / NY)
    cos = np.cos(angle) / math.sqrt(NY)
    sin = np.sin(angle) / math.sqrt(NY)
    upper = np.concatenate([cos, -sin], axis=2)
    lower = np.concatenate([sin, cos], axis=2)
    return np.concatenate([upper, lower], axis=1).astype(np.float32).astype(jnp.bfloat16)


def z_tables(block, count):
    frequency = np.arange(block)[None, :] * count + np.arange(count)[:, None]
    phase = frequency[:, :, None] * np.arange(block)[None, None, :] % NZ
    angle = phase * (two_pi / NZ)
    cos = np.cos(angle) / math.sqrt(NZ)
    sin = np.sin(angle) / math.sqrt(NZ)
    top = np.concatenate([cos, sin], axis=2)
    bottom = np.concatenate([-sin, cos], axis=2)
    return np.concatenate([top, bottom], axis=1).astype(np.float32).astype(jnp.bfloat16)


def turns(count):
    angle = np.arange(count) * (two_pi / count)
    return np.concatenate([np.cos(angle), -np.sin(angle)]).astype(np.float32)


def gather_kernel(own, parts, send, receive, local, *, wide, count, slabs, stride):
    w, n = lax.axis_index("wide"), lax.axis_index("narrow")
    chips = count // 2
    z, core = n // 2, n % 2
    other = z * 2 + (1 - core)

    def row(distance, index):
        return (distance * chips * 2 + index) * stride

    def place(distance, index):
        return parts.at[pl.ds(pl.multiple_of(row(distance, index), 8), stride), :]

    def at(distance, index):
        return receive.at[distance * count + index]

    def later(distance):
        return (w + distance) % wide

    peers = [((z + step) % chips) * 2 + core for step in range(1, chips)]
    barrier = pltpu.get_barrier_semaphore()
    for peer in peers + [other]:
        pl.semaphore_signal(
            barrier, inc=1, device_id=(w, peer), device_id_type=pl.DeviceIdType.MESH
        )
    for distance in range(1, slabs):
        pl.semaphore_signal(
            barrier,
            inc=1,
            device_id=((w + wide - distance) % wide, n),
            device_id_type=pl.DeviceIdType.MESH,
        )
    pl.semaphore_wait(barrier, chips + slabs - 1)

    sent = []

    def push(source, target, distance, index):
        copy = pltpu.make_async_remote_copy(
            src_ref=source,
            dst_ref=place(distance, index),
            send_sem=send.at[len(sent)],
            recv_sem=at(distance, index),
            device_id=target,
            device_id_type=pl.DeviceIdType.MESH,
        )
        copy.start()
        sent.append(copy)

    def arrived(distance, index):
        pltpu.make_async_remote_copy(
            src_ref=own,
            dst_ref=place(distance, index),
            send_sem=send.at[0],
            recv_sem=at(distance, index),
            device_id=(w, other),
            device_id_type=pl.DeviceIdType.MESH,
        ).wait_recv()

    for peer in peers:
        push(own, (w, peer), 0, n)
    for distance in range(1, slabs):
        push(own, (later(distance), n), distance, n)
    push(own, (w, other), 0, n)
    keep = pltpu.make_async_copy(own, place(0, n), local)
    keep.start()
    sources = [((z + chips - step) % chips) * 2 + core for step in range(chips)]
    for source in sources[1:]:
        arrived(0, source)
        for distance in range(1, slabs):
            push(place(0, source), (later(distance), n), distance, source)
        push(place(0, source), (w, other), 0, source)
    for source in sources:
        for distance in range(1, slabs):
            arrived(distance, source)
            push(place(distance, source), (w, other), distance, source)
    for distance in range(slabs):
        for chip in range(chips):
            arrived(distance, chip * 2 + (1 - core))
    for copy in sent:
        copy.wait_send()
    keep.wait()


def spectrum_kernel(
    facts, place_me, turn, parts, ztab, ytab, out, folded, order, rows,
    *, bins, block, count, stride, own_rows, slabs
):
    step = pl.program_id(0)
    window = WINDOW
    particles = parts.shape[1]

    @pl.when(step == 0)
    def _():
        folded[...] = jnp.zeros_like(folded)

        def per_device(device, total):
            def alive(state):
                b, _ = state
                return (b < bins) & (facts[device * 4 * bins + jnp.minimum(b, bins - 1)] > 0)

            def per_bin(state):
                b, total = state
                order[total] = device
                rows[total] = b
                return b + 1, total + 1

            return lax.while_loop(alive, per_bin, (0, total))[1]

        total = lax.fori_loop(0, slabs * count, per_device, 0)
        for extra in range(TOGETHER):
            order[total + extra] = 0
            rows[total + extra] = 0

        def gauss(cell, place):
            away = cell.astype(jnp.float32) - place
            return jnp.exp(-spread_rate * (away * away))

        def product(k):
            device, b = order[k], rows[k]
            r = device * stride + b * 4
            fact = device * 4 * bins + b
            x0 = device // count * XS - facts[fact + bins]
            y0 = device % count * own_rows + facts[fact + 2 * bins]
            z0 = facts[fact + 3 * bins]
            px = parts[pl.ds(r, 1), :]
            py = parts[pl.ds(r + 1, 1), :]
            pz = parts[pl.ds(r + 2, 1), :]
            force = parts[pl.ds(r + 3, 1), :]
            force = jnp.where(k < total, force, jnp.zeros_like(force))
            xi = lax.broadcasted_iota(jnp.int32, (XS, particles), 0) + x0
            along_x = jnp.where((xi >= 0) & (xi < PATCH), gauss(xi, px) * force, 0.0)
            yi = lax.broadcasted_iota(jnp.int32, (window, particles), 0) - (y0 & 7)
            along_y = jnp.where((yi >= 0) & (yi < PATCH), gauss(yi, py), 0.0)
            left = along_x[:, None, :] * along_y[None, :, :]
            left = left.reshape(XS * window, particles).astype(jnp.bfloat16)
            at = z0 & (block - 1)
            me = place_me[0]
            s0 = z0 // block * me & (count - 1)
            s1 = (z0 // block + 1) * me & (count - 1)
            zrow = lax.broadcasted_iota(jnp.int32, (block, particles), 0)
            zi = (zrow - at) & (block - 1)
            along_z = jnp.where(zi < PATCH, gauss(zi, pz), 0.0)
            first = zrow >= at
            real = along_z * jnp.where(first, turn[s0], turn[s1])
            imag = along_z * jnp.where(first, turn[count + s0], turn[count + s1])
            right = jnp.concatenate([real, imag], axis=0).astype(jnp.bfloat16)
            value = lax.dot_general(
                left, right, (((1,), (1,)), ((), ())), preferred_element_type=jnp.float32
            )
            return value.reshape(XS, window, 2 * block), pl.multiple_of(y0 // 8 * 8, 8)

        def group(g, carry):
            results = [product(g * TOGETHER + u) for u in range(TOGETHER)]
            for value, base in results:
                for h in range(2 * block // LANES):
                    folded[h, :, pl.ds(base, window), :] += value[:, :, h * LANES : (h + 1) * LANES]
            return carry

        lax.fori_loop(0, (total + TOGETHER - 1) // TOGETHER, group, 0)
        folded[:, :, :window, :] += folded[:, :, NY:, :]

    points = NY // SPLIT
    terms = []
    for t in range(SPLIT):
        lines = jnp.concatenate(
            [
                folded[h, step, pl.ds(t, points, stride=SPLIT), :].astype(jnp.bfloat16)
                for h in range(2 * block // LANES)
            ],
            axis=1,
        )
        along = lax.dot_general(
            ztab[0], lines, (((1,), (1,)), ((), ())), preferred_element_type=jnp.float32
        ).astype(jnp.bfloat16)
        along = jnp.concatenate([along[:block], along[block:]], axis=1)
        terms.append(jnp.dot(along, ytab[t], preferred_element_type=jnp.float32))
    plus, minus = terms[0] + terms[2], terms[0] - terms[2]
    odd_plus, odd_minus = terms[1] + terms[3], terms[1] - terms[3]
    low = plus + odd_plus
    high = plus - odd_plus
    out[0, 0, :, 0:points] = low[:, :points]
    out[1, 0, :, 0:points] = low[:, points:]
    out[0, 0, :, 2 * points : 3 * points] = high[:, :points]
    out[1, 0, :, 2 * points : 3 * points] = high[:, points:]
    out[0, 0, :, points : 2 * points] = minus[:, :points] + odd_minus[:, points:]
    out[1, 0, :, points : 2 * points] = minus[:, points:] - odd_minus[:, :points]
    out[0, 0, :, 3 * points :] = minus[:, :points] - odd_minus[:, points:]
    out[1, 0, :, 3 * points :] = minus[:, points:] + odd_minus[:, :points]


def body(positions, forces, counts, anchors, helpers):
    bins, _, particles = positions.shape
    count = lax.axis_size("narrow")
    wide = lax.axis_size("wide")
    me = lax.axis_index("narrow")
    block = NZ // count
    own_rows = NY // count
    slabs = 1 + (PATCH + XS - 2) // XS
    slots = slabs * count
    stride = bins * 4 + META_ROWS

    live_mask = jnp.arange(particles, dtype=jnp.int32)[None, :] < counts[:, None]
    masked = jnp.where(live_mask, forces, jnp.zeros_like(forces))
    own = jnp.concatenate([positions, masked[:, None, :]], axis=1).reshape(bins * 4, particles)
    facts = jnp.concatenate([counts[None, :], anchors, helpers.T], axis=0).astype(jnp.float32)
    facts = jnp.pad(facts, ((0, META_ROWS - facts.shape[0]), (0, particles - bins)))
    own = jnp.concatenate([own, facts], axis=0)
    parts = pl.pallas_call(
        lambda *refs: gather_kernel(*refs, wide=wide, count=count, slabs=slabs, stride=stride),
        in_specs=[pl.BlockSpec(memory_space=pltpu.VMEM)],
        out_specs=pl.BlockSpec(memory_space=pl.ANY),
        out_shape=jax.ShapeDtypeStruct((slots * stride, particles), jnp.float32),
        scratch_shapes=[
            pltpu.SemaphoreType.DMA((slots,)),
            pltpu.SemaphoreType.DMA((slots,)),
            pltpu.SemaphoreType.DMA,
        ],
        compiler_params=pltpu.CompilerParams(collective_id=0, has_side_effects=True),
        name="gather_particles",
    )(own)
    facts = parts.reshape(slots, stride, particles)[:, bins * 4 : bins * 4 + 5, :bins]
    facts = facts.astype(jnp.int32)
    mine = facts[:count, 4] == me
    load = jnp.sum(jnp.where(mine, facts[:count, 0], 0)).astype(jnp.float32) / particles
    ytab = jnp.asarray(y_tables())
    ztab = jnp.asarray(z_tables(block, count))
    turn = jnp.asarray(turns(count))

    spectrum = pl.pallas_call(
        lambda *refs: spectrum_kernel(
            *refs,
            bins=bins, block=block, count=count, stride=stride, own_rows=own_rows, slabs=slabs
        ),
        grid_spec=pltpu.PrefetchScalarGridSpec(
            num_scalar_prefetch=2,
            grid=(XS,),
            in_specs=[
                pl.BlockSpec(memory_space=pltpu.SMEM),
                pl.BlockSpec(parts.shape, lambda x, facts, me: (0, 0)),
                pl.BlockSpec((1,) + ztab.shape[1:], lambda x, facts, me: (me[0], 0, 0)),
                pl.BlockSpec(ytab.shape, lambda x, facts, me: (0, 0, 0)),
            ],
            out_specs=pl.BlockSpec((2, 1, block, NY), lambda x, facts, me: (0, x, 0, 0)),
            scratch_shapes=[
                pltpu.VMEM((2 * block // LANES, XS, NY + WINDOW, LANES), jnp.float32),
                pltpu.SMEM((slots * bins + TOGETHER,), jnp.int32),
                pltpu.SMEM((slots * bins + TOGETHER,), jnp.int32),
            ],
        ),
        out_shape=jax.ShapeDtypeStruct((2, XS, block, NY), jnp.float32),
        compiler_params=pltpu.CompilerParams(
            dimension_semantics=("arbitrary",), vmem_limit_bytes=60 * 1024 * 1024
        ),
        name="spread_and_transform",
    )(facts[:, :4].reshape(-1), me.reshape(1).astype(jnp.int32), turn, parts, ztab, ytab)
    return (spectrum, load.reshape(1, 1))


def solution(mesh):
    return jax.shard_map(
        body,
        mesh=mesh,
        in_specs=(
            P(("wide", "narrow"), None, None),
            P(("wide", "narrow"), None),
            P(("wide", "narrow")),
            P(None, ("wide", "narrow")),
            P(("wide", "narrow"), None),
        ),
        out_specs=(P(None, "wide", "narrow", None), P("wide", "narrow")),
        check_vma=False,
    )
```

```python
import math

import jax
import jax.numpy as jnp
import numpy as np
from jax import lax
from jax.experimental import pallas as pl
from jax.experimental.pallas import tpu as pltpu
from jax.sharding import PartitionSpec as P

XS = 8
NY = 1024
NZ = 1024
PATCH = 24
SPLIT = 4
WINDOW = 32
TOGETHER = 8
META_ROWS = 8
LANES = 128

spread_rate = 0.08
spread_root = math.sqrt(spread_rate / math.log(2.0))
two_pi = 2.0 * math.pi


def y_tables():
    points = NY // SPLIT
    y = np.arange(points)[None, :] * SPLIT + np.arange(SPLIT)[:, None]
    phase = (y[:, :, None] * np.arange(points)[None, None, :]) % NY
    angle = phase * (two_pi / NY)
    cos = np.cos(angle) / math.sqrt(NY)
    sin = np.sin(angle) / math.sqrt(NY)
    upper = np.concatenate([cos, -sin], axis=2)
    lower = np.concatenate([sin, cos], axis=2)
    return np.concatenate([upper, lower], axis=1).astype(np.float32).astype(jnp.bfloat16)


def z_tables(block, count):
    frequency = np.arange(block)[None, :] * count + np.arange(count)[:, None]
    phase = frequency[:, :, None] * np.arange(block)[None, None, :] % NZ
    angle = phase * (two_pi / NZ)
    cos = np.cos(angle) / math.sqrt(NZ)
    sin = np.sin(angle) / math.sqrt(NZ)
    top = np.concatenate([cos, sin], axis=2)
    bottom = np.concatenate([-sin, cos], axis=2)
    return np.concatenate([top, bottom], axis=1).astype(np.float32).astype(jnp.bfloat16)


def turns(count):
    angle = np.arange(count) * (two_pi / count)
    return np.concatenate([np.cos(angle), -np.sin(angle)]).astype(np.float32)


def gather_kernel(own, parts, send, receive, local, *, wide, count, slabs, stride):
    w, n = lax.axis_index("wide"), lax.axis_index("narrow")
    chips = count // 2
    z, core = n // 2, n % 2
    other = z * 2 + (1 - core)

    def row(distance, index):
        return (distance * chips * 2 + index) * stride

    def place(distance, index):
        return parts.at[pl.ds(pl.multiple_of(row(distance, index), 8), stride), :]

    def at(distance, index):
        return receive.at[distance * count + index]

    def later(distance):
        return (w + distance) % wide

    peers = [((z + step) % chips) * 2 + core for step in range(1, chips)]
    barrier = pltpu.get_barrier_semaphore()
    for peer in peers + [other]:
        pl.semaphore_signal(
            barrier, inc=1, device_id=(w, peer), device_id_type=pl.DeviceIdType.MESH
        )
    for distance in range(1, slabs):
        pl.semaphore_signal(
            barrier,
            inc=1,
            device_id=((w + wide - distance) % wide, n),
            device_id_type=pl.DeviceIdType.MESH,
        )
    pl.semaphore_wait(barrier, chips + slabs - 1)

    sent = []

    def push(source, target, distance, index):
        copy = pltpu.make_async_remote_copy(
            src_ref=source,
            dst_ref=place(distance, index),
            send_sem=send.at[len(sent)],
            recv_sem=at(distance, index),
            device_id=target,
            device_id_type=pl.DeviceIdType.MESH,
        )
        copy.start()
        sent.append(copy)

    def arrived(distance, index):
        pltpu.make_async_remote_copy(
            src_ref=own,
            dst_ref=place(distance, index),
            send_sem=send.at[0],
            recv_sem=at(distance, index),
            device_id=(w, other),
            device_id_type=pl.DeviceIdType.MESH,
        ).wait_recv()

    for peer in peers:
        push(own, (w, peer), 0, n)
    for distance in range(1, slabs):
        push(own, (later(distance), n), distance, n)
    push(own, (w, other), 0, n)
    keep = pltpu.make_async_copy(own, place(0, n), local)
    keep.start()
    sources = [((z + chips - step) % chips) * 2 + core for step in range(chips)]
    for source in sources[1:]:
        arrived(0, source)
        for distance in range(1, slabs):
            push(place(0, source), (later(distance), n), distance, source)
        push(place(0, source), (w, other), 0, source)
    for source in sources:
        for distance in range(1, slabs):
            arrived(distance, source)
            push(place(distance, source), (w, other), distance, source)
    for distance in range(slabs):
        for chip in range(chips):
            arrived(distance, chip * 2 + (1 - core))
    for copy in sent:
        copy.wait_send()
    keep.wait()


def spectrum_kernel(
    facts, place_me, turn, parts, ztab, ytab, out, folded, order, rows, *helds,
    bins, block, count, stride, own_rows, slabs
):
    step = pl.program_id(0)
    window = WINDOW
    particles = parts.shape[1]

    @pl.when(step == 0)
    def _():
        folded[...] = jnp.zeros_like(folded)

        def per_device(device, total):
            def alive(state):
                b, _ = state
                return (b < bins) & (facts[device * 4 * bins + jnp.minimum(b, bins - 1)] > 0)

            def per_bin(state):
                b, total = state
                order[total] = device
                rows[total] = b
                return b + 1, total + 1

            return lax.while_loop(alive, per_bin, (0, total))[1]

        total = lax.fori_loop(0, slabs * count, per_device, 0)
        for extra in range(TOGETHER):
            order[total + extra] = 0
            rows[total + extra] = 0

        def gauss(cell, place):
            away = cell.astype(jnp.float32) * spread_root - place
            return jnp.exp2(-(away * away))

        def product(k, held):
            device, b = order[k], rows[k]
            r = device * stride + b * 4
            fact = device * 4 * bins + b
            x0 = device // count * XS - facts[fact + bins]
            y0 = device % count * own_rows + facts[fact + 2 * bins]
            z0 = facts[fact + 3 * bins]
            px = parts[pl.ds(r, 1), :] * spread_root
            py = parts[pl.ds(r + 1, 1), :] * spread_root
            pz = parts[pl.ds(r + 2, 1), :] * spread_root
            force = parts[pl.ds(r + 3, 1), :]
            force = jnp.where(k < total, force, jnp.zeros_like(force))
            xi = lax.broadcasted_iota(jnp.int32, (XS, particles), 0) + x0
            along_x = jnp.where((xi >= 0) & (xi < PATCH), gauss(xi, px) * force, 0.0)
            yi = lax.broadcasted_iota(jnp.int32, (window, particles), 0) - (y0 & 7)
            along_y = jnp.where((yi >= 0) & (yi < PATCH), gauss(yi, py), 0.0)
            left = along_x[:, None, :] * along_y[None, :, :]
            left = left.reshape(XS * window, particles).astype(jnp.bfloat16)
            at = z0 & (block - 1)
            me = place_me[0]
            s0 = z0 // block * me & (count - 1)
            s1 = (z0 // block + 1) * me & (count - 1)
            zi = lax.broadcasted_iota(jnp.int32, (window, particles), 0) - (at & 7)
            inside = (zi >= 0) & (zi < PATCH)
            first = zi < block - at
            along_z = gauss(zi, pz)
            real = along_z * jnp.where(inside, jnp.where(first, turn[s0], turn[s1]), 0.0)
            imag = along_z * jnp.where(
                inside, jnp.where(first, turn[count + s0], turn[count + s1]), 0.0
            )
            starts = [
                pl.multiple_of((at // 8 * 8 + 8 * i) & (block - 1), 8) for i in range(window // 8)
            ]
            for i, start in enumerate(starts):
                held[pl.ds(start, 8), :] = real[8 * i : 8 * i + 8]
                held[pl.ds(pl.multiple_of(start + block, 8), 8), :] = imag[8 * i : 8 * i + 8]
            right = held[...].astype(jnp.bfloat16)
            for start in starts:
                held[pl.ds(start, 8), :] = jnp.zeros((8, particles), jnp.float32)
                held[pl.ds(pl.multiple_of(start + block, 8), 8), :] = jnp.zeros(
                    (8, particles), jnp.float32
                )
            value = lax.dot_general(
                left, right, (((1,), (1,)), ((), ())), preferred_element_type=jnp.float32
            )
            return value.reshape(XS, window, 2 * block), pl.multiple_of(y0 // 8 * 8, 8)

        for held in helds:
            held[...] = jnp.zeros_like(held)

        def group(g, carry):
            for u in range(TOGETHER):
                value, base = product(g * TOGETHER + u, helds[u])
                for h in range(2 * block // LANES):
                    folded[h, :, pl.ds(base, window), :] += value[:, :, h * LANES : (h + 1) * LANES]
            return carry

        lax.fori_loop(0, (total + TOGETHER - 1) // TOGETHER, group, 0)
        folded[:, :, :window, :] += folded[:, :, NY:, :]

    points = NY // SPLIT
    terms = []
    for t in range(SPLIT):
        lines = jnp.concatenate(
            [
                folded[h, step, pl.ds(t, points, stride=SPLIT), :].astype(jnp.bfloat16)
                for h in range(2 * block // LANES)
            ],
            axis=1,
        )
        along = lax.dot_general(
            ztab[0], lines, (((1,), (1,)), ((), ())), preferred_element_type=jnp.float32
        ).astype(jnp.bfloat16)
        along = jnp.concatenate([along[:block], along[block:]], axis=1)
        terms.append(jnp.dot(along, ytab[t], preferred_element_type=jnp.float32))
    plus, minus = terms[0] + terms[2], terms[0] - terms[2]
    odd_plus, odd_minus = terms[1] + terms[3], terms[1] - terms[3]
    low = plus + odd_plus
    high = plus - odd_plus
    out[0, 0, :, 0:points] = low[:, :points]
    out[1, 0, :, 0:points] = low[:, points:]
    out[0, 0, :, 2 * points : 3 * points] = high[:, :points]
    out[1, 0, :, 2 * points : 3 * points] = high[:, points:]
    out[0, 0, :, points : 2 * points] = minus[:, :points] + odd_minus[:, points:]
    out[1, 0, :, points : 2 * points] = minus[:, points:] - odd_minus[:, :points]
    out[0, 0, :, 3 * points :] = minus[:, :points] - odd_minus[:, points:]
    out[1, 0, :, 3 * points :] = minus[:, points:] + odd_minus[:, :points]


def body(positions, forces, counts, anchors, helpers):
    bins, _, particles = positions.shape
    count = lax.axis_size("narrow")
    wide = lax.axis_size("wide")
    me = lax.axis_index("narrow")
    block = NZ // count
    own_rows = NY // count
    slabs = 1 + (PATCH + XS - 2) // XS
    slots = slabs * count
    stride = bins * 4 + META_ROWS

    live_mask = jnp.arange(particles, dtype=jnp.int32)[None, :] < counts[:, None]
    masked = jnp.where(live_mask, forces, jnp.zeros_like(forces))
    own = jnp.concatenate([positions, masked[:, None, :]], axis=1).reshape(bins * 4, particles)
    facts = jnp.concatenate([counts[None, :], anchors, helpers.T], axis=0).astype(jnp.float32)
    facts = jnp.pad(facts, ((0, META_ROWS - facts.shape[0]), (0, particles - bins)))
    own = jnp.concatenate([own, facts], axis=0)
    parts = pl.pallas_call(
        lambda *refs: gather_kernel(*refs, wide=wide, count=count, slabs=slabs, stride=stride),
        in_specs=[pl.BlockSpec(memory_space=pltpu.VMEM)],
        out_specs=pl.BlockSpec(memory_space=pl.ANY),
        out_shape=jax.ShapeDtypeStruct((slots * stride, particles), jnp.float32),
        scratch_shapes=[
            pltpu.SemaphoreType.DMA((slots,)),
            pltpu.SemaphoreType.DMA((slots,)),
            pltpu.SemaphoreType.DMA,
        ],
        compiler_params=pltpu.CompilerParams(collective_id=0, has_side_effects=True),
        name="gather_particles",
    )(own)
    facts = parts.reshape(slots, stride, particles)[:, bins * 4 : bins * 4 + 5, :bins]
    facts = facts.astype(jnp.int32)
    mine = facts[:count, 4] == me
    load = jnp.sum(jnp.where(mine, facts[:count, 0], 0)).astype(jnp.float32) / particles
    ytab = jnp.asarray(y_tables())
    ztab = jnp.asarray(z_tables(block, count))
    turn = jnp.asarray(turns(count))

    spectrum = pl.pallas_call(
        lambda *refs: spectrum_kernel(
            *refs,
            bins=bins, block=block, count=count, stride=stride, own_rows=own_rows, slabs=slabs
        ),
        grid_spec=pltpu.PrefetchScalarGridSpec(
            num_scalar_prefetch=2,
            grid=(XS,),
            in_specs=[
                pl.BlockSpec(memory_space=pltpu.SMEM),
                pl.BlockSpec(parts.shape, lambda x, facts, me: (0, 0)),
                pl.BlockSpec((1,) + ztab.shape[1:], lambda x, facts, me: (me[0], 0, 0)),
                pl.BlockSpec(ytab.shape, lambda x, facts, me: (0, 0, 0)),
            ],
            out_specs=pl.BlockSpec((2, 1, block, NY), lambda x, facts, me: (0, x, 0, 0)),
            scratch_shapes=[
                pltpu.VMEM((2 * block // LANES, XS, NY + WINDOW, LANES), jnp.float32),
                pltpu.SMEM((slots * bins + TOGETHER,), jnp.int32),
                pltpu.SMEM((slots * bins + TOGETHER,), jnp.int32),
            ]
            + [pltpu.VMEM((2 * block, particles), jnp.float32)] * TOGETHER,
        ),
        out_shape=jax.ShapeDtypeStruct((2, XS, block, NY), jnp.float32),
        compiler_params=pltpu.CompilerParams(
            dimension_semantics=("arbitrary",), vmem_limit_bytes=60 * 1024 * 1024
        ),
        name="spread_and_transform",
    )(facts[:, :4].reshape(-1), me.reshape(1).astype(jnp.int32), turn, parts, ztab, ytab)
    return (spectrum, load.reshape(1, 1))


def solution(mesh):
    return jax.shard_map(
        body,
        mesh=mesh,
        in_specs=(
            P(("wide", "narrow"), None, None),
            P(("wide", "narrow"), None),
            P(("wide", "narrow")),
            P(None, ("wide", "narrow")),
            P(("wide", "narrow"), None),
        ),
        out_specs=(P(None, "wide", "narrow", None), P("wide", "narrow")),
        check_vma=False,
    )
```

```python
import math

import jax
import jax.numpy as jnp
import numpy as np
from jax import lax
from jax.experimental import pallas as pl
from jax.experimental.pallas import tpu as pltpu
from jax.sharding import PartitionSpec as P

XS = 8
NY = 1024
NZ = 1024
PATCH = 24
SPLIT = 4
WINDOW = 32
TOGETHER = 8
META_ROWS = 8
LANES = 128

spread_rate = 0.08
spread_root = math.sqrt(spread_rate / math.log(2.0))
two_pi = 2.0 * math.pi


def y_tables():
    points = NY // SPLIT
    y = np.arange(points)[None, :] * SPLIT + np.arange(SPLIT)[:, None]
    phase = (y[:, :, None] * np.arange(points)[None, None, :]) % NY
    angle = phase * (two_pi / NY)
    cos = np.cos(angle) / math.sqrt(NY)
    sin = np.sin(angle) / math.sqrt(NY)
    upper = np.concatenate([cos, -sin], axis=2)
    lower = np.concatenate([sin, cos], axis=2)
    return np.concatenate([upper, lower], axis=1).astype(np.float32).astype(jnp.bfloat16)


def z_tables(block, count):
    frequency = np.arange(block)[None, :] * count + np.arange(count)[:, None]
    phase = frequency[:, :, None] * np.arange(block)[None, None, :] % NZ
    angle = phase * (two_pi / NZ)
    cos = np.cos(angle) / math.sqrt(NZ)
    sin = np.sin(angle) / math.sqrt(NZ)
    top = np.concatenate([cos, sin], axis=2)
    bottom = np.concatenate([-sin, cos], axis=2)
    return np.concatenate([top, bottom], axis=1).astype(np.float32).astype(jnp.bfloat16)


def turns(count):
    angle = np.arange(count) * (two_pi / count)
    return np.concatenate([np.cos(angle), -np.sin(angle)]).astype(np.float32)


def gather_kernel(own, parts, send, receive, local, *, wide, count, slabs, stride):
    w, n = lax.axis_index("wide"), lax.axis_index("narrow")
    chips = count // 2
    z, core = n // 2, n % 2
    other = z * 2 + (1 - core)

    def row(distance, index):
        return (distance * chips * 2 + index) * stride

    def place(distance, index):
        return parts.at[pl.ds(pl.multiple_of(row(distance, index), 8), stride), :]

    def at(distance, index):
        return receive.at[distance * count + index]

    peers = [((z + step) % chips) * 2 + core for step in range(1, chips)]
    square = wide == 4 and slabs == 4
    if square:
        across, along = w + 1 - 2 * (w % 2), (w + 2) % wide
        near = [across, along]
        ready = near
    else:
        near = [(w + distance) % wide for distance in range(1, slabs)]
        ready = [(w + wide - distance) % wide for distance in range(1, slabs)]

    def reach(origin, target):
        return (target + wide - origin) % wide

    barrier = pltpu.get_barrier_semaphore()
    for peer in peers + [other]:
        pl.semaphore_signal(
            barrier, inc=1, device_id=(w, peer), device_id_type=pl.DeviceIdType.MESH
        )
    for target in ready:
        pl.semaphore_signal(
            barrier, inc=1, device_id=(target, n), device_id_type=pl.DeviceIdType.MESH
        )
    pl.semaphore_wait(barrier, chips + len(near))

    sent = []

    def push(source, target, distance, index):
        copy = pltpu.make_async_remote_copy(
            src_ref=source,
            dst_ref=place(distance, index),
            send_sem=send.at[len(sent)],
            recv_sem=at(distance, index),
            device_id=target,
            device_id_type=pl.DeviceIdType.MESH,
        )
        copy.start()
        sent.append(copy)

    def arrived(distance, index):
        pltpu.make_async_remote_copy(
            src_ref=own,
            dst_ref=place(distance, index),
            send_sem=send.at[0],
            recv_sem=at(distance, index),
            device_id=(w, other),
            device_id_type=pl.DeviceIdType.MESH,
        ).wait_recv()

    for peer in peers:
        push(own, (w, peer), 0, n)
    for target in near:
        push(own, (target, n), reach(w, target), n)
    push(own, (w, other), 0, n)
    keep = pltpu.make_async_copy(own, place(0, n), local)
    keep.start()
    sources = [((z + chips - step) % chips) * 2 + core for step in range(chips)]

    def forward(step, source):
        if square:
            origins = [across, along]
        else:
            origins = [(w + wide - distance) % wide for distance in range(1, slabs)]
        for turn, origin in enumerate(origins):
            distance = reach(origin, w)
            arrived(distance, source)
            if square and step % 2 == turn:
                target = near[1 - turn]
                push(place(distance, source), (target, n), reach(origin, target), source)
            push(place(distance, source), (w, other), distance, source)

    for step in range(1, chips):
        source = sources[step]
        arrived(0, source)
        for target in near:
            push(place(0, source), (target, n), reach(w, target), source)
        push(place(0, source), (w, other), 0, source)
        forward(step - 1, sources[step - 1])
    forward(chips - 1, sources[chips - 1])
    if square:
        for source in sources:
            distance = reach(3 - w, w)
            arrived(distance, source)
            push(place(distance, source), (w, other), distance, source)
    for distance in range(slabs):
        for chip in range(chips):
            arrived(distance, chip * 2 + (1 - core))
    for copy in sent:
        copy.wait_send()
    keep.wait()


def spectrum_kernel(
    facts, place_me, turn, far_parts, ztab, far_ytab, out, folded, order, rows, parts, ytab, load, *helds,
    bins, block, count, stride, own_rows, slabs
):
    step = pl.program_id(0)
    window = WINDOW
    particles = parts.shape[1]

    @pl.when(step == 0)
    def _():
        bring_parts = pltpu.make_async_copy(far_parts, parts, load.at[0])
        bring_ytab = pltpu.make_async_copy(far_ytab, ytab, load.at[1])
        bring_parts.start()
        bring_ytab.start()
        folded[...] = jnp.zeros_like(folded)

        def per_device(device, total):
            def alive(state):
                b, _ = state
                return (b < bins) & (facts[device * 4 * bins + jnp.minimum(b, bins - 1)] > 0)

            def per_bin(state):
                b, total = state
                order[total] = device
                rows[total] = b
                return b + 1, total + 1

            return lax.while_loop(alive, per_bin, (0, total))[1]

        total = lax.fori_loop(0, slabs * count, per_device, 0)
        for extra in range(TOGETHER):
            order[total + extra] = 0
            rows[total + extra] = 0

        def gauss(cell, place):
            away = cell.astype(jnp.float32) * spread_root - place
            return jnp.exp2(-(away * away))

        def product(k, held):
            device, b = order[k], rows[k]
            r = device * stride + b * 4
            fact = device * 4 * bins + b
            x0 = device // count * XS - facts[fact + bins]
            y0 = device % count * own_rows + facts[fact + 2 * bins]
            z0 = facts[fact + 3 * bins]
            px = parts[pl.ds(r, 1), :] * spread_root
            py = parts[pl.ds(r + 1, 1), :] * spread_root
            pz = parts[pl.ds(r + 2, 1), :] * spread_root
            force = parts[pl.ds(r + 3, 1), :]
            force = jnp.where(k < total, force, jnp.zeros_like(force))
            xi = lax.broadcasted_iota(jnp.int32, (XS, particles), 0) + x0
            along_x = jnp.where((xi >= 0) & (xi < PATCH), gauss(xi, px) * force, 0.0)
            yi = lax.broadcasted_iota(jnp.int32, (window, particles), 0) - (y0 & 7)
            along_y = jnp.where((yi >= 0) & (yi < PATCH), gauss(yi, py), 0.0)
            left = along_x[:, None, :] * along_y[None, :, :]
            left = left.reshape(XS * window, particles).astype(jnp.bfloat16)
            at = z0 & (block - 1)
            me = place_me[0]
            s0 = z0 // block * me & (count - 1)
            s1 = (z0 // block + 1) * me & (count - 1)
            zi = lax.broadcasted_iota(jnp.int32, (window, particles), 0) - (at & 7)
            inside = (zi >= 0) & (zi < PATCH)
            first = zi < block - at
            along_z = gauss(zi, pz)
            real = along_z * jnp.where(inside, jnp.where(first, turn[s0], turn[s1]), 0.0)
            imag = along_z * jnp.where(
                inside, jnp.where(first, turn[count + s0], turn[count + s1]), 0.0
            )
            starts = [
                pl.multiple_of((at // 8 * 8 + 8 * i) & (block - 1), 8) for i in range(window // 8)
            ]
            for i, start in enumerate(starts):
                held[pl.ds(start, 8), :] = real[8 * i : 8 * i + 8]
                held[pl.ds(pl.multiple_of(start + block, 8), 8), :] = imag[8 * i : 8 * i + 8]
            right = held[...].astype(jnp.bfloat16)
            for start in starts:
                held[pl.ds(start, 8), :] = jnp.zeros((8, particles), jnp.float32)
                held[pl.ds(pl.multiple_of(start + block, 8), 8), :] = jnp.zeros(
                    (8, particles), jnp.float32
                )
            value = lax.dot_general(
                left, right, (((1,), (1,)), ((), ())), preferred_element_type=jnp.float32
            )
            return value.reshape(XS, window, 2 * block), pl.multiple_of(y0 // 8 * 8, 8)

        for held in helds:
            held[...] = jnp.zeros_like(held)
        bring_parts.wait()

        def group(g, carry):
            for u in range(TOGETHER):
                value, base = product(g * TOGETHER + u, helds[u])
                for h in range(2 * block // LANES):
                    folded[h, :, pl.ds(base, window), :] += value[:, :, h * LANES : (h + 1) * LANES]
            return carry

        lax.fori_loop(0, (total + TOGETHER - 1) // TOGETHER, group, 0)
        folded[:, :, :window, :] += folded[:, :, NY:, :]
        bring_ytab.wait()

    points = NY // SPLIT
    terms = []
    for t in range(SPLIT):
        lines = jnp.concatenate(
            [
                folded[h, step, pl.ds(t, points, stride=SPLIT), :].astype(jnp.bfloat16)
                for h in range(2 * block // LANES)
            ],
            axis=1,
        )
        along = lax.dot_general(
            ztab[0], lines, (((1,), (1,)), ((), ())), preferred_element_type=jnp.float32
        ).astype(jnp.bfloat16)
        along = jnp.concatenate([along[:block], along[block:]], axis=1)
        terms.append(jnp.dot(along, ytab[t], preferred_element_type=jnp.float32))
    plus, minus = terms[0] + terms[2], terms[0] - terms[2]
    odd_plus, odd_minus = terms[1] + terms[3], terms[1] - terms[3]
    low = plus + odd_plus
    high = plus - odd_plus
    out[0, 0, :, 0:points] = low[:, :points]
    out[1, 0, :, 0:points] = low[:, points:]
    out[0, 0, :, 2 * points : 3 * points] = high[:, :points]
    out[1, 0, :, 2 * points : 3 * points] = high[:, points:]
    out[0, 0, :, points : 2 * points] = minus[:, :points] + odd_minus[:, points:]
    out[1, 0, :, points : 2 * points] = minus[:, points:] - odd_minus[:, :points]
    out[0, 0, :, 3 * points :] = minus[:, :points] - odd_minus[:, points:]
    out[1, 0, :, 3 * points :] = minus[:, points:] + odd_minus[:, :points]


def body(positions, forces, counts, anchors, helpers):
    bins, _, particles = positions.shape
    count = lax.axis_size("narrow")
    wide = lax.axis_size("wide")
    me = lax.axis_index("narrow")
    block = NZ // count
    own_rows = NY // count
    slabs = 1 + (PATCH + XS - 2) // XS
    slots = slabs * count
    stride = bins * 4 + META_ROWS

    live_mask = jnp.arange(particles, dtype=jnp.int32)[None, :] < counts[:, None]
    masked = jnp.where(live_mask, forces, jnp.zeros_like(forces))
    own = jnp.concatenate([positions, masked[:, None, :]], axis=1).reshape(bins * 4, particles)
    facts = jnp.concatenate([counts[None, :], anchors, helpers.T], axis=0).astype(jnp.float32)
    facts = jnp.pad(facts, ((0, META_ROWS - facts.shape[0]), (0, particles - bins)))
    own = jnp.concatenate([own, facts], axis=0)
    parts = pl.pallas_call(
        lambda *refs: gather_kernel(*refs, wide=wide, count=count, slabs=slabs, stride=stride),
        in_specs=[pl.BlockSpec(memory_space=pltpu.VMEM)],
        out_specs=pl.BlockSpec(memory_space=pl.ANY),
        out_shape=jax.ShapeDtypeStruct((slots * stride, particles), jnp.float32),
        scratch_shapes=[
            pltpu.SemaphoreType.DMA((slots,)),
            pltpu.SemaphoreType.DMA((slots,)),
            pltpu.SemaphoreType.DMA,
        ],
        compiler_params=pltpu.CompilerParams(collective_id=0, has_side_effects=True),
        name="gather_particles",
    )(own)
    facts = parts.reshape(slots, stride, particles)[:, bins * 4 : bins * 4 + 5, :bins]
    facts = facts.astype(jnp.int32)
    mine = facts[:count, 4] == me
    load = jnp.sum(jnp.where(mine, facts[:count, 0], 0)).astype(jnp.float32) / particles
    ytab = jnp.asarray(y_tables())
    ztab = jnp.asarray(z_tables(block, count))
    turn = jnp.asarray(turns(count))

    spectrum = pl.pallas_call(
        lambda *refs: spectrum_kernel(
            *refs,
            bins=bins, block=block, count=count, stride=stride, own_rows=own_rows, slabs=slabs
        ),
        grid_spec=pltpu.PrefetchScalarGridSpec(
            num_scalar_prefetch=2,
            grid=(XS,),
            in_specs=[
                pl.BlockSpec(memory_space=pltpu.SMEM),
                pl.BlockSpec(memory_space=pl.ANY),
                pl.BlockSpec((1,) + ztab.shape[1:], lambda x, facts, me: (me[0], 0, 0)),
                pl.BlockSpec(memory_space=pl.ANY),
            ],
            out_specs=pl.BlockSpec((2, 1, block, NY), lambda x, facts, me: (0, x, 0, 0)),
            scratch_shapes=[
                pltpu.VMEM((2 * block // LANES, XS, NY + WINDOW, LANES), jnp.float32),
                pltpu.SMEM((slots * bins + TOGETHER,), jnp.int32),
                pltpu.SMEM((slots * bins + TOGETHER,), jnp.int32),
                pltpu.VMEM(parts.shape, jnp.float32),
                pltpu.VMEM(ytab.shape, jnp.bfloat16),
                pltpu.SemaphoreType.DMA((2,)),
            ]
            + [pltpu.VMEM((2 * block, particles), jnp.float32)] * TOGETHER,
        ),
        out_shape=jax.ShapeDtypeStruct((2, XS, block, NY), jnp.float32),
        compiler_params=pltpu.CompilerParams(
            dimension_semantics=("arbitrary",), vmem_limit_bytes=60 * 1024 * 1024
        ),
        name="spread_and_transform",
    )(facts[:, :4].reshape(-1), me.reshape(1).astype(jnp.int32), turn, parts, ztab, ytab)
    return (spectrum, load.reshape(1, 1))


def solution(mesh):
    return jax.shard_map(
        body,
        mesh=mesh,
        in_specs=(
            P(("wide", "narrow"), None, None),
            P(("wide", "narrow"), None),
            P(("wide", "narrow")),
            P(None, ("wide", "narrow")),
            P(("wide", "narrow"), None),
        ),
        out_specs=(P(None, "wide", "narrow", None), P("wide", "narrow")),
        check_vma=False,
    )
```
